256 devices in a mesh: los: 16 (over x_lo, z), tile: 16 (over x_hi, y, core).
Axes of the slice: x: 4 (x_hi: 2, x_lo: 2; x = x_hi * 2 + x_lo), y: 4, z: 8, core: 2. Of those that a mesh axis runs over, the one named last changes fastest.
Arguments:
- density: bfloat16 [128, 512, 2048], P('tile', None, 'los'), may hold values from -18 to 18
- direction: bfloat16 [128, 512, 2048], P('tile', None, 'los'), may hold values from -6 to 6
- inverse_variance: bfloat16 [128, 512, 2048], P('tile', None, 'los'), may hold values from 0.25 to 4
- pixel_mask: int32 [128, 512, 2048], P('tile', None, 'los'), may hold values 0 or 1
- slot_count: int32 [16, 16], P('los', 'tile'), may hold values from 32 to 128, as said below
- slot_group: int32 [16, 16, 128], P('los', 'tile'), may hold values from 0 to 31
- slot_shift: int32 [16, 16, 128], P('los', 'tile'), may hold values from -1 to 1
- block_tiles: bfloat16 [16, 16, 128, 128, 128], P('los', 'tile'), as said below
Outputs:
- hessian_product: float32 [128, 512, 2048], P('tile', None, 'los')
The draws below stay inside these ranges and needn't reach their ends.
Inputs may be any that keep to these rules, and one draw needn't show every extreme that they name: Only the first slot_count slots of a device's lists are used; the rest are ignored. `slot_shift`: A shift of -1 names the previous slab and 1 the next, wrapping around the sightline. `block_tiles`: entries are nonnegative.
All inputs are finite; a program needn't handle non-finite values. No bound on the sum of `pixel_mask` on one device may be relied on, other than what follows from the above.
Results may differ from the reference program's by a relative error of at most 0.0081.
Values may be sent and summed in bfloat16 or wider, within the bound.
A program may use at most 128 MiB of HBM per device.

```python
import math
import jax
import jax.numpy as jnp
from jax import lax

XT_DEV = 8
TY = 512
LOS_DEV = 128
GROUP = 128
SIGMA = 2
REACH = 6
GROUPS = 32
SLOTS = 128
NX = 128
NL = 2048
N_LOS = 16
N_TILE = 16


def draw_slot_count(key, part):
    key_base, key_high, key_low = jax.random.split(key, 3)
    devices_total = N_LOS * N_TILE
    counts_flat = jax.random.randint(key_base, (devices_total,), SLOTS // 4, SLOTS + 1)
    high_index = jax.random.randint(key_high, (), 0, devices_total)
    low_index = (high_index + 1 + jax.random.randint(key_low, (), 0, devices_total - 1)) % devices_total
    counts_flat = counts_flat.at[high_index].set(SLOTS).at[low_index].set(SLOTS // 4)
    return counts_flat.reshape(N_LOS, N_TILE).astype(jnp.int32)


def draw_block_tiles(key, part):
    key_shift, key_width, key_rough = jax.random.split(jax.random.fold_in(key, 17), 3)
    lead = (N_LOS, N_TILE, SLOTS)
    velocity = jax.random.uniform(key_shift, lead + (1, 1), jnp.float32, -0.25 * LOS_DEV, 0.25 * LOS_DEV)
    spread = jax.random.uniform(key_width, lead + (1, 1), jnp.float32, 1.5, 4.0)
    source = jnp.arange(LOS_DEV).astype(jnp.float32)[:, None]
    target = jnp.arange(LOS_DEV).astype(jnp.float32)[None, :]
    offset = target - source - velocity
    profile = jnp.exp(-offset * offset / (2.0 * spread * spread)) / (2.5066283 * spread)
    rough = jax.random.uniform(key_rough, lead + (LOS_DEV, LOS_DEV), jnp.float32, 0.5, 1.5)
    return (profile * rough).astype(jnp.bfloat16)


def place_ends(array, stream_key, least, high):
    longest = array.shape.index(max(array.shape))
    spots = []
    for shift in (0, 1):
        where = [jax.random.randint(jax.random.fold_in(stream_key, axis), (), 0, length) for axis, length in enumerate(array.shape)]
        where[longest] = (where[longest] + shift) % array.shape[longest]
        spots.append(tuple(where))
    return array.at[spots[0]].set(least).at[spots[1]].set(high)


def steps_of(stream_key, extent, cuts, least, top_value):
    factor_of, own = 1.0, jax.random.fold_in(stream_key, 6)
    for dim, shards_of in cuts:
        heights = jnp.exp(jax.random.uniform(jax.random.fold_in(own, dim), (shards_of,), jnp.float32, least / len(cuts), top_value / len(cuts)))
        factor_of = factor_of * jnp.repeat(heights, extent[dim] // shards_of).reshape([-1 if axis == dim else 1 for axis in range(len(extent))])
    return factor_of


def bell_draw(rng, dims, width, limit, pieces=(), dtype=jnp.bfloat16):
    factor_of = steps_of(rng, dims, pieces, -0.22, 0.18) if pieces else 1.0
    entries = jax.random.normal(rng, dims, jnp.float32) * width * factor_of
    return jnp.minimum(jnp.maximum(entries, -limit), limit).astype(dtype)


def setup_inputs(seed: int = 0) -> dict:
    key_list = jax.random.split(jax.random.key(seed), 9)
    density = bell_draw(key_list[0], (NX, TY, NL), 3.0, 18.0, ((0, 16), (2, 16)))
    direction = bell_draw(key_list[1], (NX, TY, NL), 1.0, 6.0, ((0, 16), (2, 16)))
    inverse_variance = jnp.clip(jnp.exp(math.log(4.0) - 2.7725887 * jax.random.uniform(key_list[2], (NX, TY, NL), jnp.float32) ** steps_of(key_list[2], (NX, TY, NL), ((0, 16), (2, 16)), -0.2, 0.2)), 0.25, 4.0).astype(jnp.bfloat16)
    pixel_mask = place_ends((jax.random.randint(key_list[3], (NX, TY, NL), 0, 4) < 3).astype(jnp.int32), jax.random.fold_in(key_list[3], 1), 0, 1)
    slot_count = draw_slot_count(jax.random.fold_in(key_list[8], 71), 0)
    slot_group = place_ends(jax.random.randint(key_list[5], (N_LOS, N_TILE, SLOTS), 0, GROUPS), jax.random.fold_in(key_list[5], 1), 0, GROUPS - 1).astype(jnp.int32)
    slot_shift = place_ends(jax.random.randint(key_list[6], (N_LOS, N_TILE, SLOTS), -1, 2), jax.random.fold_in(key_list[6], 1), -1, 1).astype(jnp.int32)
    block_tiles = draw_block_tiles(jax.random.fold_in(key_list[8], 71), 0)
    return dict(density=density, direction=direction, inverse_variance=inverse_variance, pixel_mask=pixel_mask, slot_count=slot_count, slot_group=slot_group, slot_shift=slot_shift, block_tiles=block_tiles)


def kernel_weights(spacing):
    inside = jnp.abs(spacing) <= REACH
    values = jnp.where(inside, jnp.exp(-spacing * spacing / (2.0 * SIGMA * SIGMA)), 0.0)
    span = jnp.arange(-REACH, REACH + 1).astype(jnp.float32)
    normal = jnp.sum(jnp.exp(-span * span / (2.0 * SIGMA * SIGMA)))
    return values / normal


def row_kernel():
    position = jnp.arange(NX).astype(jnp.int32)
    differ = jnp.mod(position[:, None] - position[None, :], NX)
    spacing = jnp.minimum(differ, NX - differ).astype(jnp.float32)
    return kernel_weights(spacing).astype(jnp.bfloat16).astype(jnp.float32)


def column_kernel():
    position = jnp.arange(TY).astype(jnp.int32)
    spacing = (position[:, None] - position[None, :]).astype(jnp.float32)
    return kernel_weights(spacing).astype(jnp.bfloat16).astype(jnp.float32)


def to_blocks(field):
    shaped = field.reshape(N_TILE, XT_DEV, TY, N_LOS, LOS_DEV).transpose(3, 0, 1, 2, 4)
    return shaped.reshape(N_LOS * N_TILE, GROUPS, GROUP, LOS_DEV)


def from_blocks(blocks):
    shaped = blocks.reshape(N_LOS, N_TILE, XT_DEV, TY, LOS_DEV).transpose(1, 2, 3, 0, 4)
    return shaped.reshape(NX, TY, NL)


def redistribute(items):
    sources, count, groups_list, shifts, tiles = items
    chosen = ((shifts + 1) * GROUPS + groups_list).astype(jnp.int32)
    picked = jnp.take(sources, chosen, axis=1).astype(jnp.float32)
    product = jnp.einsum("csgb,sbd->csgd", picked, tiles.astype(jnp.float32), precision=lax.Precision.HIGHEST)
    live = (jnp.arange(SLOTS).astype(jnp.int32) < count).astype(jnp.float32)
    placing = (groups_list[:, None] == jnp.arange(GROUPS).astype(jnp.int32)[None, :]).astype(jnp.float32) * live[:, None]
    return jnp.einsum("sn,csgd->cngd", placing, product, precision=lax.Precision.HIGHEST)


def gather_back(items):
    adjoint, count, groups_list, shifts, tiles = items
    picked = jnp.take(adjoint, groups_list.astype(jnp.int32), axis=0).astype(jnp.float32)
    product = jnp.einsum("sgd,sbd->sgb", picked, tiles.astype(jnp.float32), precision=lax.Precision.HIGHEST)
    chosen = ((shifts + 1) * GROUPS + groups_list).astype(jnp.int32)
    live = (jnp.arange(SLOTS).astype(jnp.int32) < count).astype(jnp.float32)
    placing = (chosen[:, None] == jnp.arange(3 * GROUPS).astype(jnp.int32)[None, :]).astype(jnp.float32) * live[:, None]
    return jnp.einsum("sn,sgb->ngb", placing, product, precision=lax.Precision.HIGHEST)


def smooth_field(stack, rows_matrix, cols_matrix):
    row_smooth = jnp.einsum("ap,cpyl->cayl", rows_matrix, stack.astype(jnp.float32), precision=lax.Precision.HIGHEST).astype(jnp.bfloat16)
    return jnp.einsum("zy,cayl->cazl", cols_matrix, row_smooth.astype(jnp.float32), precision=lax.Precision.HIGHEST)


def reference(density, direction, inverse_variance, pixel_mask, slot_count, slot_group, slot_shift, block_tiles):
    rows_matrix = row_kernel()
    cols_matrix = column_kernel()
    smooth = smooth_field(jnp.stack([density, direction]), rows_matrix, cols_matrix)
    tau_real = 0.5 * jnp.exp(1.6 * smooth[0])
    tangent = (1.6 * tau_real * smooth[1]).astype(jnp.bfloat16)
    tau_half = tau_real.astype(jnp.bfloat16)
    pair_blocks = jnp.stack([to_blocks(tau_half), to_blocks(tangent)], axis=1)
    shaped = pair_blocks.reshape((N_LOS, N_TILE) + pair_blocks.shape[1:])
    before = jnp.roll(shaped, 1, axis=0)
    after = jnp.roll(shaped, -1, axis=0)
    sources = jnp.concatenate([before, shaped, after], axis=3)
    sources = sources.reshape((N_LOS * N_TILE,) + sources.shape[2:])
    counts = slot_count.reshape(N_LOS * N_TILE)
    groups_all = slot_group.reshape(N_LOS * N_TILE, SLOTS)
    shifts_all = slot_shift.reshape(N_LOS * N_TILE, SLOTS)
    tiles_all = block_tiles.reshape(N_LOS * N_TILE, SLOTS, LOS_DEV, LOS_DEV)
    redshift = lax.map(redistribute, (sources, counts, groups_all, shifts_all, tiles_all))
    tau_z = from_blocks(redshift[:, 0])
    dtau = from_blocks(redshift[:, 1])
    flux = jnp.exp(-tau_z)
    weight = pixel_mask.astype(jnp.float32) * inverse_variance.astype(jnp.float32)
    adjoint_flux = (weight * flux * flux * dtau).astype(jnp.bfloat16)
    parts = lax.map(gather_back, (to_blocks(adjoint_flux), counts, groups_all, shifts_all, tiles_all))
    parts = parts.reshape((N_LOS, N_TILE) + parts.shape[1:])
    lower = parts[:, :, :GROUPS]
    middle = parts[:, :, GROUPS:2 * GROUPS]
    upper = parts[:, :, 2 * GROUPS:]
    adjoint_blocks = middle + jnp.roll(upper, 1, axis=0) + jnp.roll(lower, -1, axis=0)
    adjoint_real = from_blocks(adjoint_blocks)
    pulled = (1.6 * tau_real * adjoint_real).astype(jnp.bfloat16)
    return smooth_field(pulled[None], rows_matrix, cols_matrix)[0]
```

```python
import jax
import jax.numpy as jnp
import numpy as np
from jax import lax
from jax.experimental import pallas as pl
from jax.experimental.pallas import tpu as pltpu
from jax.sharding import PartitionSpec as P

MESH = pl.DeviceIdType.MESH
GROUP = 128
SIGMA = 2
REACH = 6
ROWS = 8
WIDTH = 512
PIX = 128
SLOTS = 128
GROUPS = 32
PAD = 16
CUTS = (0, 128, 256, 384, 512)
SCALE = 2.0**-7
BF = jnp.bfloat16
F32 = jnp.float32


def taps():
    span = np.arange(-REACH, REACH + 1).astype(np.float32)
    values = np.exp(-span * span / np.float32(2.0 * SIGMA * SIGMA)).astype(np.float32)
    held = (values / values.sum(dtype=np.float32)).astype(BF).astype(np.float32)
    return [float(v) for v in held[REACH:]]


def smooth_rows_block(weights, get, put):
    rows = [get(r).astype(F32) for r in range(ROWS + 2 * REACH)]
    for a in range(ROWS):
        mid = a + REACH
        total = weights[0] * rows[mid]
        for k in range(1, REACH + 1):
            total = total + weights[k] * (rows[mid - k] + rows[mid + k])
        put(a, total.astype(BF))


def body(
    cuts,
    cnt_ref,
    grp_ref,
    shf_ref,
    den_ref,
    dir_ref,
    iv_ref,
    msk_ref,
    til_ref,
    out_ref,
    own,
    lo,
    hi,
    rs,
    kc,
    tau,
    mine,
    left,
    right,
    til,
    acc,
    wts,
    tabv,
    tabs,
    iv,
    msk,
    inner,
    send_l,
    send_r,
    got_l,
    got_r,
    pul,
    plo,
    phi,
    br,
    outv,
    load_sem,
    tab_sem,
    p1_send,
    p1_recv,
    p2_send,
    p2_recv,
    p4_send,
    p4_recv,
    p5_send,
    p5_recv,
    out_sem,
):
    n = len(cuts) - 1
    ycut = [0] + [z + PAD for z in cuts[1:-1]] + [WIDTH]
    vcut = [0] + [z - PAD for z in cuts[1:-1]] + [WIDTH]
    los, tile = lax.axis_index("los"), lax.axis_index("tile")
    n_los, n_tile = lax.axis_size("los"), lax.axis_size("tile")
    nxt = (lax.rem(los + 1, n_los), tile)
    prv = (lax.rem(los + n_los - 1, n_los), tile)
    up = (los, lax.rem(tile + 1, n_tile))
    down = (los, lax.rem(tile + n_tile - 1, n_tile))
    w = taps()

    barrier = pltpu.get_barrier_semaphore()
    for other in (nxt, prv, up, down):
        pl.semaphore_signal(barrier, inc=1, device_id=other, device_id_type=MESH)
    pl.semaphore_wait(barrier, 4)

    def remote(src, dst, send, recv, device):
        return pltpu.make_async_remote_copy(
            src_ref=src,
            dst_ref=dst,
            send_sem=send,
            recv_sem=recv,
            device_id=device,
            device_id_type=MESH,
        )

    p1 = []
    for c in range(n):
        ys = pl.ds(ycut[c], ycut[c + 1] - ycut[c])
        copies = []
        for f, src in enumerate((den_ref, dir_ref)):
            copies.append(
                remote(
                    src.at[pl.ds(ROWS - REACH, REACH), ys],
                    lo.at[f, :, ys],
                    p1_send.at[c, f, 0],
                    p1_recv.at[c, f, 0],
                    up,
                )
            )
            copies.append(
                remote(
                    src.at[pl.ds(0, REACH), ys],
                    hi.at[f, :, ys],
                    p1_send.at[c, f, 1],
                    p1_recv.at[c, f, 1],
                    down,
                )
            )
        for copy in copies:
            copy.start()
        p1.append(copies)
    loads = [
        pltpu.make_async_copy(den_ref, own.at[0], load_sem.at[0]),
        pltpu.make_async_copy(dir_ref, own.at[1], load_sem.at[1]),
        pltpu.make_async_copy(til_ref, til, load_sem.at[2]),
        pltpu.make_async_copy(iv_ref, iv, load_sem.at[3]),
        pltpu.make_async_copy(msk_ref, msk, load_sem.at[4]),
    ]
    for load in loads:
        load.start()

    lane = lax.broadcasted_iota(jnp.int32, (SLOTS, SLOTS), 1)
    sub = lax.broadcasted_iota(jnp.int32, (SLOTS, SLOTS), 0)
    count = cnt_ref[0, 0]
    key = (shf_ref[...] + 1) * GROUPS + grp_ref[...]
    key = jnp.where(lax.broadcasted_iota(jnp.int32, (1, SLOTS), 1) < count, key, -1)
    key_row = jnp.broadcast_to(key, (SLOTS, SLOTS))
    key_col = jnp.transpose(key_row)

    def highest(found):
        x = jnp.where(found, sub, -1)
        size = SLOTS
        while size > 8:
            size //= 2
            x = jnp.maximum(x[:size], x[size:])
        for shift in (4, 2, 1):
            x = jnp.maximum(x, pltpu.roll(x, shift, 0))
        return jnp.where(x < 0, SLOTS, x)

    tabv[0] = highest((key_col == key_row) & (sub < lane))
    tabv[1] = highest(key_col == lane)
    to_smem = pltpu.make_async_copy(tabv, tabs, tab_sem)
    to_smem.start()

    rows_i = lax.broadcasted_iota(jnp.int32, kc.shape, 0)
    cols_i = lax.broadcasted_iota(jnp.int32, kc.shape, 1)
    apart = jnp.abs(rows_i + PAD - cols_i)
    band = jnp.zeros(kc.shape, F32)
    for k in range(REACH + 1):
        band = jnp.where(apart == k, w[k], band)
    kc[...] = band.astype(BF)
    for a in range(ROWS):
        for edge in (0, PAD + WIDTH):
            for f in range(2):
                rs[f, a, pl.ds(edge, PAD)] = jnp.zeros((PAD, PIX), BF)
            br[a, pl.ds(edge, PAD)] = jnp.zeros((PAD, PIX), BF)

    loads[0].wait()
    loads[1].wait()

    p2 = []
    for c in range(n):
        for copy in p1[c]:
            copy.wait_recv()

        @pl.loop(0, (ycut[c + 1] - ycut[c]) // 16)
        def _(i, y0=ycut[c]):
            y = pl.multiple_of(y0 + i * 16, 16)
            for f in range(2):

                def get(r):
                    if r < REACH:
                        return lo[f, r, pl.ds(y, 16)]
                    if r < REACH + ROWS:
                        return own[f, r - REACH, pl.ds(y, 16)]
                    return hi[f, r - REACH - ROWS, pl.ds(y, 16)]

                def put(a, value):
                    rs[f, a, pl.ds(y + PAD, 16)] = value

                smooth_rows_block(w, get, put)

        z0, m = cuts[c], cuts[c + 1] - cuts[c]
        zs = pl.ds(z0, m)

        @pl.loop(0, ROWS)
        def _(a, z0=z0, m=m, zs=zs):
            both = jnp.concatenate(
                [rs[0, a, pl.ds(z0, m + 2 * PAD)], rs[1, a, pl.ds(z0, m + 2 * PAD)]], axis=1
            )
            su = jnp.dot(kc[:m, : m + 2 * PAD], both, preferred_element_type=F32)
            t = 0.5 * jnp.exp(1.6 * su[:, :PIX])
            tau[a, zs] = t
            mine[a, 0, zs] = t.astype(BF)
            mine[a, 1, zs] = (1.6 * t * su[:, PIX:]).astype(BF)

        copies = [
            remote(mine.at[:, :, zs], left.at[:, :, zs], p2_send.at[c, 0], p2_recv.at[c, 0], nxt),
            remote(mine.at[:, :, zs], right.at[:, :, zs], p2_send.at[c, 1], p2_recv.at[c, 1], prv),
        ]
        for copy in copies:
            copy.start()
        p2.append(copies)

    loads[2].wait()
    to_smem.wait()
    acc[SLOTS] = jnp.zeros((PIX, PIX), F32)

    @pl.loop(0, SLOTS)
    def _(q):
        acc[q] = til[q].astype(F32) * SCALE + acc[tabs[0, 0, q]]

    @pl.loop(0, 3 * GROUPS)
    def _(i):
        wts[i] = acc[tabs[1, 0, i]].astype(BF)

    loads[3].wait()
    loads[4].wait()

    p4 = []
    per_row = WIDTH // GROUP
    for c in range(n):
        for copy in p2[c]:
            copy.wait_recv()
        z0, m = cuts[c], cuts[c + 1] - cuts[c]
        zs = pl.ds(z0, m)

        @pl.loop(0, ROWS)
        def _(a, zs=zs, m=m, part=z0 // GROUP):
            g = a * per_row + part
            total = None
            for o, ref in enumerate((left, mine, right)):
                block = jnp.concatenate([ref[a, 0, zs], ref[a, 1, zs]], axis=0)
                term = jnp.dot(block, wts[o * GROUPS + g], preferred_element_type=F32)
                total = term if total is None else total + term
            total = total * (1.0 / SCALE)
            flux = jnp.exp(-total[:m])
            weight = msk[a, zs].astype(F32) * iv[a, zs].astype(F32)
            adjoint = (weight * flux * flux * total[m:]).astype(BF)
            back = [
                lax.dot_general(
                    adjoint,
                    wts[o * GROUPS + g],
                    (((1,), (1,)), ((), ())),
                    preferred_element_type=F32,
                )
                * (1.0 / SCALE)
                for o in range(3)
            ]
            send_l[a, zs] = back[0].astype(BF)
            inner[a, zs] = back[1]
            send_r[a, zs] = back[2].astype(BF)

        copies = [
            remote(send_r.at[:, zs], got_l.at[:, zs], p4_send.at[c, 0], p4_recv.at[c, 0], nxt),
            remote(send_l.at[:, zs], got_r.at[:, zs], p4_send.at[c, 1], p4_recv.at[c, 1], prv),
        ]
        for copy in copies:
            copy.start()
        p4.append(copies)

    p5 = []
    outs = []

    def finish(c):
        for copy in p5[c]:
            copy.wait_recv()

        @pl.loop(0, (cuts[c + 1] - cuts[c]) // 16)
        def _(i):
            y = pl.multiple_of(cuts[c] + i * 16, 16)

            def get(r):
                if r < REACH:
                    return plo[r, pl.ds(y, 16)]
                if r < REACH + ROWS:
                    return pul[r - REACH, pl.ds(y, 16)]
                return phi[r - REACH - ROWS, pl.ds(y, 16)]

            def put(a, value):
                br[a, pl.ds(y + PAD, 16)] = value

            smooth_rows_block(w, get, put)

        v0, m = vcut[c], vcut[c + 1] - vcut[c]

        @pl.loop(0, ROWS)
        def _(a):
            outv[a, pl.ds(v0, m)] = jnp.dot(
                kc[:m, : m + 2 * PAD], br[a, pl.ds(v0, m + 2 * PAD)], preferred_element_type=F32
            )

        copy = pltpu.make_async_copy(
            outv.at[:, pl.ds(v0, m)], out_ref.at[:, pl.ds(v0, m)], out_sem.at[c]
        )
        copy.start()
        outs.append(copy)

    for c in range(n):
        for copy in p4[c]:
            copy.wait_recv()
        zs = pl.ds(cuts[c], cuts[c + 1] - cuts[c])

        @pl.loop(0, ROWS)
        def _(a, zs=zs):
            real = inner[a, zs] + got_l[a, zs].astype(F32) + got_r[a, zs].astype(F32)
            pul[a, zs] = (1.6 * tau[a, zs] * real).astype(BF)

        copies = [
            remote(
                pul.at[pl.ds(ROWS - REACH, REACH), zs],
                plo.at[:, zs],
                p5_send.at[c, 0],
                p5_recv.at[c, 0],
                up,
            ),
            remote(
                pul.at[pl.ds(0, REACH), zs], phi.at[:, zs], p5_send.at[c, 1], p5_recv.at[c, 1], down
            ),
        ]
        for copy in copies:
            copy.start()
        p5.append(copies)
        if c:
            finish(c - 1)
    finish(n - 1)
    for group in (p1, p2, p4, p5):
        for copies in group:
            for copy in copies:
                copy.wait_send()
    for copy in outs:
        copy.wait()


def on_device(
    density,
    direction,
    inverse_variance,
    pixel_mask,
    slot_count,
    slot_group,
    slot_shift,
    block_tiles,
):
    cuts = CUTS
    n = len(cuts) - 1
    tallest = max([b - a for a, b in zip(cuts, cuts[1:])] + [WIDTH - cuts[-2] + PAD])
    any_spec = pl.BlockSpec(memory_space=pl.ANY)
    vmem = pl.BlockSpec(memory_space=pltpu.VMEM)
    dma = pltpu.SemaphoreType.DMA

    def kernel(*refs):
        body(cuts, *refs)

    return pl.pallas_call(
        kernel,
        name="hessian_product",
        out_shape=jax.ShapeDtypeStruct((ROWS, WIDTH, PIX), F32),
        in_specs=[
            pl.BlockSpec(memory_space=pltpu.SMEM),
            vmem,
            vmem,
            any_spec,
            any_spec,
            any_spec,
            any_spec,
            any_spec,
        ],
        out_specs=any_spec,
        scratch_shapes=[
            pltpu.VMEM((2, ROWS, WIDTH, PIX), BF),
            pltpu.VMEM((2, REACH, WIDTH, PIX), BF),
            pltpu.VMEM((2, REACH, WIDTH, PIX), BF),
            pltpu.VMEM((2, ROWS, WIDTH + 2 * PAD, PIX), BF),
            pltpu.VMEM((tallest, 256), BF),
            pltpu.VMEM((ROWS, WIDTH, PIX), F32),
            pltpu.VMEM((ROWS, 2, WIDTH, PIX), BF),
            pltpu.VMEM((ROWS, 2, WIDTH, PIX), BF),
            pltpu.VMEM((ROWS, 2, WIDTH, PIX), BF),
            pltpu.VMEM((SLOTS, PIX, PIX), BF),
            pltpu.VMEM((SLOTS + 1, PIX, PIX), F32),
            pltpu.VMEM((3 * GROUPS, PIX, PIX), BF),
            pltpu.VMEM((2, 8, SLOTS), jnp.int32),
            pltpu.SMEM((2, 8, SLOTS), jnp.int32),
            pltpu.VMEM((ROWS, WIDTH, PIX), BF),
            pltpu.VMEM((ROWS, WIDTH, PIX), jnp.int32),
            pltpu.VMEM((ROWS, WIDTH, PIX), F32),
            pltpu.VMEM((ROWS, WIDTH, PIX), BF),
            pltpu.VMEM((ROWS, WIDTH, PIX), BF),
            pltpu.VMEM((ROWS, WIDTH, PIX), BF),
            pltpu.VMEM((ROWS, WIDTH, PIX), BF),
            pltpu.VMEM((ROWS, WIDTH, PIX), BF),
            pltpu.VMEM((REACH, WIDTH, PIX), BF),
            pltpu.VMEM((REACH, WIDTH, PIX), BF),
            pltpu.VMEM((ROWS, WIDTH + 2 * PAD, PIX), BF),
            pltpu.VMEM((ROWS, WIDTH, PIX), F32),
            dma((5,)),
            dma,
            dma((n, 2, 2)),
            dma((n, 2, 2)),
            dma((n, 2)),
            dma((n, 2)),
            dma((n, 2)),
            dma((n, 2)),
            dma((n, 2)),
            dma((n, 2)),
            dma((n,)),
        ],
        compiler_params=pltpu.CompilerParams(
            collective_id=0, has_side_effects=True, vmem_limit_bytes=62 * 1024 * 1024
        ),
    )(
        slot_count,
        slot_group[0],
        slot_shift[0],
        density,
        direction,
        inverse_variance,
        pixel_mask,
        block_tiles[0, 0],
    )


def solution(mesh):
    placed = (
        P("tile", None, "los"),
        P("tile", None, "los"),
        P("tile", None, "los"),
        P("tile", None, "los"),
        P("los", "tile"),
        P("los", "tile", None),
        P("los", "tile", None),
        P("los", "tile", None, None, None),
    )
    return jax.shard_map(
        on_device, mesh=mesh, in_specs=placed, out_specs=P("tile", None, "los"), check_vma=False
    )
```

```python
import jax
import jax.numpy as jnp
import numpy as np
from jax import lax
from jax.experimental import pallas as pl
from jax.experimental.pallas import tpu as pltpu
from jax.sharding import PartitionSpec as P

MESH = pl.DeviceIdType.MESH
GROUP = 128
SIGMA = 2
REACH = 6
ROWS = 8
WIDTH = 512
PIX = 128
SLOTS = 128
GROUPS = 32
PAD = 16
CUTS = (0, 128, 256, 384, 512)
SCALE = 2.0**-7
BF = jnp.bfloat16
F32 = jnp.float32


def taps():
    span = np.arange(-REACH, REACH + 1).astype(np.float32)
    values = np.exp(-span * span / np.float32(2.0 * SIGMA * SIGMA)).astype(np.float32)
    held = (values / values.sum(dtype=np.float32)).astype(BF).astype(np.float32)
    return [float(v) for v in held[REACH:]]


def smooth_rows_block(weights, get, put):
    rows = [get(r).astype(F32) for r in range(ROWS + 2 * REACH)]
    for a in range(ROWS):
        mid = a + REACH
        total = weights[0] * rows[mid]
        for k in range(1, REACH + 1):
            total = total + weights[k] * (rows[mid - k] + rows[mid + k])
        put(a, total.astype(BF))


def body(
    cuts,
    cnt_ref,
    grp_ref,
    shf_ref,
    den_ref,
    dir_ref,
    iv_ref,
    msk_ref,
    til_ref,
    out_ref,
    own,
    lo,
    hi,
    rs,
    kc,
    tau,
    mine,
    left,
    right,
    til,
    acc,
    wts,
    tabv,
    tabs,
    iv,
    msk,
    inner,
    send_l,
    send_r,
    got_l,
    got_r,
    pul,
    plo,
    phi,
    br,
    outv,
    load_sem,
    tab_sem,
    p1_send,
    p1_recv,
    p2_send,
    p2_recv,
    p4_send,
    p4_recv,
    p5_send,
    p5_recv,
    out_sem,
):
    n = len(cuts) - 1
    ycut = [0] + [z + PAD for z in cuts[1:-1]] + [WIDTH]
    vcut = [0] + [z - PAD for z in cuts[1:-1]] + [WIDTH]
    los, tile = lax.axis_index("los"), lax.axis_index("tile")
    n_los, n_tile = lax.axis_size("los"), lax.axis_size("tile")
    nxt = (lax.rem(los + 1, n_los), tile)
    prv = (lax.rem(los + n_los - 1, n_los), tile)
    up = (los, lax.rem(tile + 1, n_tile))
    down = (los, lax.rem(tile + n_tile - 1, n_tile))
    w = taps()
    place = lax.rem(tile, 8)
    shared = (place < 2) | (place > 5)
    ends = lax.rem(los, 8)
    late = (shared & (ends == 7), shared & (ends == 0))

    barrier = pltpu.get_barrier_semaphore()
    for other in (nxt, prv, up, down):
        pl.semaphore_signal(barrier, inc=1, device_id=other, device_id_type=MESH)
    pl.semaphore_wait(barrier, 4)

    def remote(src, dst, send, recv, device):
        return pltpu.make_async_remote_copy(
            src_ref=src,
            dst_ref=dst,
            send_sem=send,
            recv_sem=recv,
            device_id=device,
            device_id_type=MESH,
        )

    p1 = []
    for c in range(n):
        ys = pl.ds(ycut[c], ycut[c + 1] - ycut[c])
        copies = []
        for f, src in enumerate((den_ref, dir_ref)):
            copies.append(
                remote(
                    src.at[pl.ds(ROWS - REACH, REACH), ys],
                    lo.at[f, :, ys],
                    p1_send.at[c, f, 0],
                    p1_recv.at[c, f, 0],
                    up,
                )
            )
            copies.append(
                remote(
                    src.at[pl.ds(0, REACH), ys],
                    hi.at[f, :, ys],
                    p1_send.at[c, f, 1],
                    p1_recv.at[c, f, 1],
                    down,
                )
            )
        for copy in copies:
            copy.start()
        p1.append(copies)
    loads = [
        pltpu.make_async_copy(den_ref, own.at[0], load_sem.at[0]),
        pltpu.make_async_copy(dir_ref, own.at[1], load_sem.at[1]),
        pltpu.make_async_copy(til_ref, til, load_sem.at[2]),
        pltpu.make_async_copy(iv_ref, iv, load_sem.at[3]),
        pltpu.make_async_copy(msk_ref, msk, load_sem.at[4]),
    ]
    for load in loads:
        load.start()

    lane = lax.broadcasted_iota(jnp.int32, (SLOTS, SLOTS), 1)
    sub = lax.broadcasted_iota(jnp.int32, (SLOTS, SLOTS), 0)
    count = cnt_ref[0, 0]
    key = (shf_ref[...] + 1) * GROUPS + grp_ref[...]
    key = jnp.where(lax.broadcasted_iota(jnp.int32, (1, SLOTS), 1) < count, key, -1)
    key_row = jnp.broadcast_to(key, (SLOTS, SLOTS))
    key_col = jnp.transpose(key_row)

    def highest(found):
        x = jnp.where(found, sub, -1)
        size = SLOTS
        while size > 8:
            size //= 2
            x = jnp.maximum(x[:size], x[size:])
        for shift in (4, 2, 1):
            x = jnp.maximum(x, pltpu.roll(x, shift, 0))
        return jnp.where(x < 0, SLOTS, x)

    tabv[0] = highest((key_col == key_row) & (sub < lane))
    tabv[1] = highest(key_col == lane)
    to_smem = pltpu.make_async_copy(tabv, tabs, tab_sem)
    to_smem.start()

    rows_i = lax.broadcasted_iota(jnp.int32, kc.shape, 0)
    cols_i = lax.broadcasted_iota(jnp.int32, kc.shape, 1)
    apart = jnp.abs(rows_i + PAD - cols_i)
    band = jnp.zeros(kc.shape, F32)
    for k in range(REACH + 1):
        band = jnp.where(apart == k, w[k], band)
    kc[...] = band.astype(BF)
    for a in range(ROWS):
        for edge in (0, PAD + WIDTH):
            for f in range(2):
                rs[f, a, pl.ds(edge, PAD)] = jnp.zeros((PAD, PIX), BF)
            br[a, pl.ds(edge, PAD)] = jnp.zeros((PAD, PIX), BF)

    loads[0].wait()
    loads[1].wait()

    p2 = []
    for c in range(n):
        for copy in p1[c]:
            copy.wait_recv()

        @pl.loop(0, (ycut[c + 1] - ycut[c]) // 16)
        def _(i, y0=ycut[c]):
            y = pl.multiple_of(y0 + i * 16, 16)
            for f in range(2):

                def get(r):
                    if r < REACH:
                        return lo[f, r, pl.ds(y, 16)]
                    if r < REACH + ROWS:
                        return own[f, r - REACH, pl.ds(y, 16)]
                    return hi[f, r - REACH - ROWS, pl.ds(y, 16)]

                def put(a, value):
                    rs[f, a, pl.ds(y + PAD, 16)] = value

                smooth_rows_block(w, get, put)

        z0, m = cuts[c], cuts[c + 1] - cuts[c]
        zs = pl.ds(z0, m)

        @pl.loop(0, ROWS)
        def _(a, z0=z0, m=m, zs=zs):
            both = jnp.concatenate(
                [rs[0, a, pl.ds(z0, m + 2 * PAD)], rs[1, a, pl.ds(z0, m + 2 * PAD)]], axis=1
            )
            su = jnp.dot(kc[:m, : m + 2 * PAD], both, preferred_element_type=F32)
            t = 0.5 * jnp.exp(1.6 * su[:, :PIX])
            tau[a, zs] = t
            mine[a, 0, zs] = t.astype(BF)
            mine[a, 1, zs] = (1.6 * t * su[:, PIX:]).astype(BF)

        copies = [
            remote(mine.at[:, :, zs], left.at[:, :, zs], p2_send.at[c, 0], p2_recv.at[c, 0], nxt),
            remote(mine.at[:, :, zs], right.at[:, :, zs], p2_send.at[c, 1], p2_recv.at[c, 1], prv),
        ]
        for held, copy in zip(late, copies):
            pl.when(jnp.logical_not(held))(copy.start)
        p2.append(copies)
    for copies in p2:
        for held, copy in zip(late, copies):
            pl.when(held)(copy.start)

    loads[2].wait()
    to_smem.wait()
    acc[SLOTS] = jnp.zeros((PIX, PIX), F32)

    @pl.loop(0, SLOTS)
    def _(q):
        acc[q] = til[q].astype(F32) * SCALE + acc[tabs[0, 0, q]]

    @pl.loop(0, 3 * GROUPS)
    def _(i):
        wts[i] = acc[tabs[1, 0, i]].astype(BF)

    loads[3].wait()
    loads[4].wait()

    p4 = []
    per_row = WIDTH // GROUP
    for c in range(n):
        for copy in p2[c]:
            copy.wait_recv()
        z0, m = cuts[c], cuts[c + 1] - cuts[c]
        zs = pl.ds(z0, m)

        @pl.loop(0, ROWS)
        def _(a, zs=zs, m=m, part=z0 // GROUP):
            g = a * per_row + part
            total = None
            for o, ref in enumerate((left, mine, right)):
                block = jnp.concatenate([ref[a, 0, zs], ref[a, 1, zs]], axis=0)
                term = jnp.dot(block, wts[o * GROUPS + g], preferred_element_type=F32)
                total = term if total is None else total + term
            total = total * (1.0 / SCALE)
            flux = jnp.exp(-total[:m])
            weight = msk[a, zs].astype(F32) * iv[a, zs].astype(F32)
            adjoint = (weight * flux * flux * total[m:]).astype(BF)
            back = [
                lax.dot_general(
                    adjoint,
                    wts[o * GROUPS + g],
                    (((1,), (1,)), ((), ())),
                    preferred_element_type=F32,
                )
                * (1.0 / SCALE)
                for o in range(3)
            ]
            send_l[a, zs] = back[0].astype(BF)
            inner[a, zs] = back[1]
            send_r[a, zs] = back[2].astype(BF)

        copies = [
            remote(send_r.at[:, zs], got_l.at[:, zs], p4_send.at[c, 0], p4_recv.at[c, 0], nxt),
            remote(send_l.at[:, zs], got_r.at[:, zs], p4_send.at[c, 1], p4_recv.at[c, 1], prv),
        ]
        for copy in copies:
            copy.start()
        p4.append(copies)

    p5 = []
    outs = []

    def finish(c):
        for copy in p5[c]:
            copy.wait_recv()

        @pl.loop(0, (cuts[c + 1] - cuts[c]) // 16)
        def _(i):
            y = pl.multiple_of(cuts[c] + i * 16, 16)

            def get(r):
                if r < REACH:
                    return plo[r, pl.ds(y, 16)]
                if r < REACH + ROWS:
                    return pul[r - REACH, pl.ds(y, 16)]
                return phi[r - REACH - ROWS, pl.ds(y, 16)]

            def put(a, value):
                br[a, pl.ds(y + PAD, 16)] = value

            smooth_rows_block(w, get, put)

        v0, m = vcut[c], vcut[c + 1] - vcut[c]

        @pl.loop(0, ROWS)
        def _(a):
            outv[a, pl.ds(v0, m)] = jnp.dot(
                kc[:m, : m + 2 * PAD], br[a, pl.ds(v0, m + 2 * PAD)], preferred_element_type=F32
            )

        copy = pltpu.make_async_copy(
            outv.at[:, pl.ds(v0, m)], out_ref.at[:, pl.ds(v0, m)], out_sem.at[c]
        )
        copy.start()
        outs.append(copy)

    for c in range(n):
        for copy in p4[c]:
            copy.wait_recv()
        zs = pl.ds(cuts[c], cuts[c + 1] - cuts[c])

        @pl.loop(0, ROWS)
        def _(a, zs=zs):
            real = inner[a, zs] + got_l[a, zs].astype(F32) + got_r[a, zs].astype(F32)
            pul[a, zs] = (1.6 * tau[a, zs] * real).astype(BF)

        copies = [
            remote(
                pul.at[pl.ds(ROWS - REACH, REACH), zs],
                plo.at[:, zs],
                p5_send.at[c, 0],
                p5_recv.at[c, 0],
                up,
            ),
            remote(
                pul.at[pl.ds(0, REACH), zs], phi.at[:, zs], p5_send.at[c, 1], p5_recv.at[c, 1], down
            ),
        ]
        for copy in copies:
            copy.start()
        p5.append(copies)
        if c:
            finish(c - 1)
    finish(n - 1)
    for group in (p1, p2, p4, p5):
        for copies in group:
            for copy in copies:
                copy.wait_send()
    for copy in outs:
        copy.wait()


def on_device(
    density,
    direction,
    inverse_variance,
    pixel_mask,
    slot_count,
    slot_group,
    slot_shift,
    block_tiles,
):
    cuts = CUTS
    n = len(cuts) - 1
    tallest = max([b - a for a, b in zip(cuts, cuts[1:])] + [WIDTH - cuts[-2] + PAD])
    any_spec = pl.BlockSpec(memory_space=pl.ANY)
    vmem = pl.BlockSpec(memory_space=pltpu.VMEM)
    dma = pltpu.SemaphoreType.DMA

    def kernel(*refs):
        body(cuts, *refs)

    return pl.pallas_call(
        kernel,
        name="hessian_product",
        out_shape=jax.ShapeDtypeStruct((ROWS, WIDTH, PIX), F32),
        in_specs=[
            pl.BlockSpec(memory_space=pltpu.SMEM),
            vmem,
            vmem,
            any_spec,
            any_spec,
            any_spec,
            any_spec,
            any_spec,
        ],
        out_specs=any_spec,
        scratch_shapes=[
            pltpu.VMEM((2, ROWS, WIDTH, PIX), BF),
            pltpu.VMEM((2, REACH, WIDTH, PIX), BF),
            pltpu.VMEM((2, REACH, WIDTH, PIX), BF),
            pltpu.VMEM((2, ROWS, WIDTH + 2 * PAD, PIX), BF),
            pltpu.VMEM((tallest, 256), BF),
            pltpu.VMEM((ROWS, WIDTH, PIX), F32),
            pltpu.VMEM((ROWS, 2, WIDTH, PIX), BF),
            pltpu.VMEM((ROWS, 2, WIDTH, PIX), BF),
            pltpu.VMEM((ROWS, 2, WIDTH, PIX), BF),
            pltpu.VMEM((SLOTS, PIX, PIX), BF),
            pltpu.VMEM((SLOTS + 1, PIX, PIX), F32),
            pltpu.VMEM((3 * GROUPS, PIX, PIX), BF),
            pltpu.VMEM((2, 8, SLOTS), jnp.int32),
            pltpu.SMEM((2, 8, SLOTS), jnp.int32),
            pltpu.VMEM((ROWS, WIDTH, PIX), BF),
            pltpu.VMEM((ROWS, WIDTH, PIX), jnp.int32),
            pltpu.VMEM((ROWS, WIDTH, PIX), F32),
            pltpu.VMEM((ROWS, WIDTH, PIX), BF),
            pltpu.VMEM((ROWS, WIDTH, PIX), BF),
            pltpu.VMEM((ROWS, WIDTH, PIX), BF),
            pltpu.VMEM((ROWS, WIDTH, PIX), BF),
            pltpu.VMEM((ROWS, WIDTH, PIX), BF),
            pltpu.VMEM((REACH, WIDTH, PIX), BF),
            pltpu.VMEM((REACH, WIDTH, PIX), BF),
            pltpu.VMEM((ROWS, WIDTH + 2 * PAD, PIX), BF),
            pltpu.VMEM((ROWS, WIDTH, PIX), F32),
            dma((5,)),
            dma,
            dma((n, 2, 2)),
            dma((n, 2, 2)),
            dma((n, 2)),
            dma((n, 2)),
            dma((n, 2)),
            dma((n, 2)),
            dma((n, 2)),
            dma((n, 2)),
            dma((n,)),
        ],
        compiler_params=pltpu.CompilerParams(
            collective_id=0, has_side_effects=True, vmem_limit_bytes=62 * 1024 * 1024
        ),
    )(
        slot_count,
        slot_group[0],
        slot_shift[0],
        density,
        direction,
        inverse_variance,
        pixel_mask,
        block_tiles[0, 0],
    )


def solution(mesh):
    placed = (
        P("tile", None, "los"),
        P("tile", None, "los"),
        P("tile", None, "los"),
        P("tile", None, "los"),
        P("los", "tile"),
        P("los", "tile", None),
        P("los", "tile", None),
        P("los", "tile", None, None, None),
    )
    return jax.shard_map(
        on_device, mesh=mesh, in_specs=placed, out_specs=P("tile", None, "los"), check_vma=False
    )
```

```python
import jax
import jax.numpy as jnp
import numpy as np
from jax import lax
from jax.experimental import pallas as pl
from jax.experimental.pallas import tpu as pltpu
from jax.sharding import PartitionSpec as P

MESH = pl.DeviceIdType.MESH
GROUP = 128
SIGMA = 2
REACH = 6
ROWS = 8
WIDTH = 512
PIX = 128
SLOTS = 128
GROUPS = 32
PAD = 16
CUTS = (0, 128, 256, 384, 512)
SCALE = 2.0**-7
RELAYED = (0, 1)
BF = jnp.bfloat16
F32 = jnp.float32


def taps():
    span = np.arange(-REACH, REACH + 1).astype(np.float32)
    values = np.exp(-span * span / np.float32(2.0 * SIGMA * SIGMA)).astype(np.float32)
    held = (values / values.sum(dtype=np.float32)).astype(BF).astype(np.float32)
    return [float(v) for v in held[REACH:]]


def smooth_rows_block(weights, get, put):
    rows = [get(r).astype(F32) for r in range(ROWS + 2 * REACH)]
    for a in range(ROWS):
        mid = a + REACH
        total = weights[0] * rows[mid]
        for k in range(1, REACH + 1):
            total = total + weights[k] * (rows[mid - k] + rows[mid + k])
        put(a, total.astype(BF))


def body(
    cuts,
    cnt_ref,
    grp_ref,
    shf_ref,
    den_ref,
    dir_ref,
    iv_ref,
    msk_ref,
    til_ref,
    out_ref,
    own,
    lo,
    hi,
    rs,
    kc,
    tau,
    mine,
    left,
    right,
    til,
    acc,
    wts,
    tabv,
    tabs,
    iv,
    msk,
    inner,
    send_l,
    send_r,
    got_l,
    got_r,
    pul,
    plo,
    phi,
    br,
    outv,
    load_sem,
    tab_sem,
    p1_send,
    p1_recv,
    p2_send,
    p2_recv,
    p4_send,
    p4_recv,
    p5_send,
    p5_recv,
    out_sem,
    rout,
    hop_send,
    hop_recv,
):
    n = len(cuts) - 1
    ycut = [0] + [z + PAD for z in cuts[1:-1]] + [WIDTH]
    vcut = [0] + [z - PAD for z in cuts[1:-1]] + [WIDTH]
    los, tile = lax.axis_index("los"), lax.axis_index("tile")
    n_los, n_tile = lax.axis_size("los"), lax.axis_size("tile")
    nxt = (lax.rem(los + 1, n_los), tile)
    prv = (lax.rem(los + n_los - 1, n_los), tile)
    up = (los, lax.rem(tile + 1, n_tile))
    down = (los, lax.rem(tile + n_tile - 1, n_tile))
    w = taps()
    place, end = lax.rem(tile, n_tile // 2), lax.rem(los, n_los // 2)
    shared = (place < 2) | (place > 5)
    late = (shared & (end == n_los // 2 - 1), shared & (end == 0))
    at_end = (end == n_los // 2 - 1) | (end == 0)
    from_up, from_down = at_end & (place == 7), at_end & (place == 0)
    relay_up, relay_down = at_end & (place == 5), at_end & (place == 2)

    def across(step):
        return (lax.rem(los + n_los // 2, n_los), lax.rem(tile + step, n_tile))

    partners = (
        (from_up, (6, 11)),
        (from_down, (10, 5)),
        (relay_up, (10, 11)),
        (relay_down, (6, 5)),
    )

    barrier = pltpu.get_barrier_semaphore()
    for other in (nxt, prv, up, down):
        pl.semaphore_signal(barrier, inc=1, device_id=other, device_id_type=MESH)
    for role, steps in partners:

        @pl.when(role)
        def _(steps=steps):
            for step in steps:
                pl.semaphore_signal(barrier, inc=1, device_id=across(step), device_id_type=MESH)

    involved = from_up | from_down | relay_up | relay_down
    pl.semaphore_wait(barrier, jnp.where(involved, 6, 4))

    def remote(src, dst, send, recv, device):
        return pltpu.make_async_remote_copy(
            src_ref=src,
            dst_ref=dst,
            send_sem=send,
            recv_sem=recv,
            device_id=device,
            device_id_type=MESH,
        )

    high, low = pl.ds(ROWS - REACH, REACH), pl.ds(0, REACH)

    def launch(role, direct, via):
        if via is None:
            direct.start()
        else:
            pl.when(role)(via.start)
            pl.when(jnp.logical_not(role))(direct.start)

    p1 = []
    for c in range(n):
        ys = pl.ds(ycut[c], ycut[c + 1] - ycut[c])
        copies = []
        for f, src in enumerate((den_ref, dir_ref)):
            for d, (rows, dst, device) in enumerate(((high, lo, up), (low, hi, down))):
                copies.append(
                    remote(
                        src.at[rows, ys],
                        dst.at[f, :, ys],
                        p1_send.at[c, f, d],
                        p1_recv.at[c, f, d],
                        device,
                    )
                )
        for copy in copies:
            copy.start()
        p1.append(copies)

    def pass_on(arrivals, onward):
        for role, copies in zip((relay_up, relay_down), onward):

            @pl.when(role)
            def _(copies=copies):
                for arrival, copy in zip(arrivals, copies):
                    arrival.wait_recv()
                    copy.start()

    def passed(arrivals, onward):
        for role, copies in zip((relay_up, relay_down), onward):

            @pl.when(role)
            def _(copies=copies):
                for copy in copies:
                    copy.wait_send()

    loads = [
        pltpu.make_async_copy(den_ref, own.at[0], load_sem.at[0]),
        pltpu.make_async_copy(dir_ref, own.at[1], load_sem.at[1]),
        pltpu.make_async_copy(til_ref, til, load_sem.at[2]),
        pltpu.make_async_copy(iv_ref, iv, load_sem.at[3]),
        pltpu.make_async_copy(msk_ref, msk, load_sem.at[4]),
    ]
    for load in loads:
        load.start()

    lane = lax.broadcasted_iota(jnp.int32, (SLOTS, SLOTS), 1)
    sub = lax.broadcasted_iota(jnp.int32, (SLOTS, SLOTS), 0)
    count = cnt_ref[0, 0]
    key = (shf_ref[...] + 1) * GROUPS + grp_ref[...]
    key = jnp.where(lax.broadcasted_iota(jnp.int32, (1, SLOTS), 1) < count, key, -1)
    key_row = jnp.broadcast_to(key, (SLOTS, SLOTS))
    key_col = jnp.transpose(key_row)

    def highest(found):
        x = jnp.where(found, sub, -1)
        size = SLOTS
        while size > 8:
            size //= 2
            x = jnp.maximum(x[:size], x[size:])
        for shift in (4, 2, 1):
            x = jnp.maximum(x, pltpu.roll(x, shift, 0))
        return jnp.where(x < 0, SLOTS, x)

    tabv[0] = highest((key_col == key_row) & (sub < lane))
    tabv[1] = highest(key_col == lane)
    to_smem = pltpu.make_async_copy(tabv, tabs, tab_sem)
    to_smem.start()

    rows_i = lax.broadcasted_iota(jnp.int32, kc.shape, 0)
    cols_i = lax.broadcasted_iota(jnp.int32, kc.shape, 1)
    apart = jnp.abs(rows_i + PAD - cols_i)
    band = jnp.zeros(kc.shape, F32)
    for k in range(REACH + 1):
        band = jnp.where(apart == k, w[k], band)
    kc[...] = band.astype(BF)
    for a in range(ROWS):
        for edge in (0, PAD + WIDTH):
            for f in range(2):
                rs[f, a, pl.ds(edge, PAD)] = jnp.zeros((PAD, PIX), BF)
            br[a, pl.ds(edge, PAD)] = jnp.zeros((PAD, PIX), BF)

    loads[0].wait()
    loads[1].wait()

    p2 = []
    for c in range(n):
        for copy in p1[c]:
            copy.wait_recv()
        if c == n - 1:
            for copies in p2:
                for held, copy in zip(late, copies):
                    pl.when(held)(copy.start)

        @pl.loop(0, (ycut[c + 1] - ycut[c]) // 16)
        def _(i, y0=ycut[c]):
            y = pl.multiple_of(y0 + i * 16, 16)
            for f in range(2):

                def get(r):
                    if r < REACH:
                        return lo[f, r, pl.ds(y, 16)]
                    if r < REACH + ROWS:
                        return own[f, r - REACH, pl.ds(y, 16)]
                    return hi[f, r - REACH - ROWS, pl.ds(y, 16)]

                def put(a, value):
                    rs[f, a, pl.ds(y + PAD, 16)] = value

                smooth_rows_block(w, get, put)

        z0, m = cuts[c], cuts[c + 1] - cuts[c]
        zs = pl.ds(z0, m)

        @pl.loop(0, ROWS)
        def _(a, z0=z0, m=m, zs=zs):
            both = jnp.concatenate(
                [rs[0, a, pl.ds(z0, m + 2 * PAD)], rs[1, a, pl.ds(z0, m + 2 * PAD)]], axis=1
            )
            su = jnp.dot(kc[:m, : m + 2 * PAD], both, preferred_element_type=F32)
            t = 0.5 * jnp.exp(1.6 * su[:, :PIX])
            tau[a, zs] = t
            mine[a, 0, zs] = t.astype(BF)
            mine[a, 1, zs] = (1.6 * t * su[:, PIX:]).astype(BF)

        copies = [
            remote(mine.at[:, :, zs], left.at[:, :, zs], p2_send.at[c, 0], p2_recv.at[c, 0], nxt),
            remote(mine.at[:, :, zs], right.at[:, :, zs], p2_send.at[c, 1], p2_recv.at[c, 1], prv),
        ]
        p2.append(copies)
        for d, held in enumerate(late):
            if c < n - 1:
                pl.when(jnp.logical_not(held))(copies[d].start)
            else:
                copies[d].start()

    loads[2].wait()
    to_smem.wait()
    acc[SLOTS] = jnp.zeros((PIX, PIX), F32)

    @pl.loop(0, SLOTS)
    def _(q):
        acc[q] = til[q].astype(F32) * SCALE + acc[tabs[0, 0, q]]

    @pl.loop(0, 3 * GROUPS)
    def _(i):
        wts[i] = acc[tabs[1, 0, i]].astype(BF)

    loads[3].wait()
    loads[4].wait()

    p4 = []
    per_row = WIDTH // GROUP
    for c in range(n):
        for copy in p2[c]:
            copy.wait_recv()
        z0, m = cuts[c], cuts[c + 1] - cuts[c]
        zs = pl.ds(z0, m)

        @pl.loop(0, ROWS)
        def _(a, zs=zs, m=m, part=z0 // GROUP):
            g = a * per_row + part
            total = None
            for o, ref in enumerate((left, mine, right)):
                block = jnp.concatenate([ref[a, 0, zs], ref[a, 1, zs]], axis=0)
                term = jnp.dot(block, wts[o * GROUPS + g], preferred_element_type=F32)
                total = term if total is None else total + term
            total = total * (1.0 / SCALE)
            flux = jnp.exp(-total[:m])
            weight = msk[a, zs].astype(F32) * iv[a, zs].astype(F32)
            adjoint = (weight * flux * flux * total[m:]).astype(BF)
            back = [
                lax.dot_general(
                    adjoint,
                    wts[o * GROUPS + g],
                    (((1,), (1,)), ((), ())),
                    preferred_element_type=F32,
                )
                * (1.0 / SCALE)
                for o in range(3)
            ]
            send_l[a, zs] = back[0].astype(BF)
            inner[a, zs] = back[1]
            send_r[a, zs] = back[2].astype(BF)

        copies = [
            remote(send_r.at[:, zs], got_l.at[:, zs], p4_send.at[c, 0], p4_recv.at[c, 0], nxt),
            remote(send_l.at[:, zs], got_r.at[:, zs], p4_send.at[c, 1], p4_recv.at[c, 1], prv),
        ]
        for copy in copies:
            copy.start()
        p4.append(copies)

    p5 = []
    outs = []
    back = []

    def finish(c):
        for copy in p5[c]:
            copy.wait_recv()

        @pl.loop(0, (cuts[c + 1] - cuts[c]) // 16)
        def _(i):
            y = pl.multiple_of(cuts[c] + i * 16, 16)

            def get(r):
                if r < REACH:
                    return plo[r, pl.ds(y, 16)]
                if r < REACH + ROWS:
                    return pul[r - REACH, pl.ds(y, 16)]
                return phi[r - REACH - ROWS, pl.ds(y, 16)]

            def put(a, value):
                br[a, pl.ds(y + PAD, 16)] = value

            smooth_rows_block(w, get, put)

        v0, m = vcut[c], vcut[c + 1] - vcut[c]

        @pl.loop(0, ROWS)
        def _(a):
            outv[a, pl.ds(v0, m)] = jnp.dot(
                kc[:m, : m + 2 * PAD], br[a, pl.ds(v0, m + 2 * PAD)], preferred_element_type=F32
            )

        copy = pltpu.make_async_copy(
            outv.at[:, pl.ds(v0, m)], out_ref.at[:, pl.ds(v0, m)], out_sem.at[c]
        )
        copy.start()
        outs.append(copy)

    for c in range(n):
        for copy in p4[c]:
            copy.wait_recv()
        zs = pl.ds(cuts[c], cuts[c + 1] - cuts[c])

        @pl.loop(0, ROWS)
        def _(a, zs=zs):
            real = inner[a, zs] + got_l[a, zs].astype(F32) + got_r[a, zs].astype(F32)
            pul[a, zs] = (1.6 * tau[a, zs] * real).astype(BF)

        copies, arrivals, onward = [], [], ([], [])
        for d, (rows, dst, device, role, step) in enumerate(
            ((high, plo, up, from_up, 6), (low, phi, down, from_down, 10))
        ):
            sems = (p5_send.at[c, d], p5_recv.at[c, d])
            direct = remote(pul.at[rows, zs], dst.at[:, zs], *sems, device)
            via = None
            if c in RELAYED:
                kept = rout.at[:, zs]
                via = remote(pul.at[rows, zs], kept, sems[0], hop_recv.at[c], across(step))
                goal = across((11, 5)[d])
                onward[d].append(remote(kept, dst.at[:, zs], hop_send.at[c], sems[1], goal))
                if d == 0:
                    arrivals.append(via)
            launch(role, direct, via)
            copies.append(direct)
        p5.append(copies)
        if arrivals:
            back.append((arrivals, onward))
    for relayed in back:
        pass_on(*relayed)
    for c in range(n):
        finish(c)
    for group in (p1, p2, p4, p5):
        for copies in group:
            for copy in copies:
                copy.wait_send()
    for relayed in back:
        passed(*relayed)
    for copy in outs:
        copy.wait()


def on_device(
    density,
    direction,
    inverse_variance,
    pixel_mask,
    slot_count,
    slot_group,
    slot_shift,
    block_tiles,
):
    cuts = CUTS
    n = len(cuts) - 1
    tallest = max([b - a for a, b in zip(cuts, cuts[1:])] + [WIDTH - cuts[-2] + PAD])
    any_spec = pl.BlockSpec(memory_space=pl.ANY)
    vmem = pl.BlockSpec(memory_space=pltpu.VMEM)
    dma = pltpu.SemaphoreType.DMA

    def kernel(*refs):
        body(cuts, *refs)

    return pl.pallas_call(
        kernel,
        name="hessian_product",
        out_shape=jax.ShapeDtypeStruct((ROWS, WIDTH, PIX), F32),
        in_specs=[
            pl.BlockSpec(memory_space=pltpu.SMEM),
            vmem,
            vmem,
            any_spec,
            any_spec,
            any_spec,
            any_spec,
            any_spec,
        ],
        out_specs=any_spec,
        scratch_shapes=[
            pltpu.VMEM((2, ROWS, WIDTH, PIX), BF),
            pltpu.VMEM((2, REACH, WIDTH, PIX), BF),
            pltpu.VMEM((2, REACH, WIDTH, PIX), BF),
            pltpu.VMEM((2, ROWS, WIDTH + 2 * PAD, PIX), BF),
            pltpu.VMEM((tallest, 256), BF),
            pltpu.VMEM((ROWS, WIDTH, PIX), F32),
            pltpu.VMEM((ROWS, 2, WIDTH, PIX), BF),
            pltpu.VMEM((ROWS, 2, WIDTH, PIX), BF),
            pltpu.VMEM((ROWS, 2, WIDTH, PIX), BF),
            pltpu.VMEM((SLOTS, PIX, PIX), BF),
            pltpu.VMEM((SLOTS + 1, PIX, PIX), F32),
            pltpu.VMEM((3 * GROUPS, PIX, PIX), BF),
            pltpu.VMEM((2, 8, SLOTS), jnp.int32),
            pltpu.SMEM((2, 8, SLOTS), jnp.int32),
            pltpu.VMEM((ROWS, WIDTH, PIX), BF),
            pltpu.VMEM((ROWS, WIDTH, PIX), jnp.int32),
            pltpu.VMEM((ROWS, WIDTH, PIX), F32),
            pltpu.VMEM((ROWS, WIDTH, PIX), BF),
            pltpu.VMEM((ROWS, WIDTH, PIX), BF),
            pltpu.VMEM((ROWS, WIDTH, PIX), BF),
            pltpu.VMEM((ROWS, WIDTH, PIX), BF),
            pltpu.VMEM((ROWS, WIDTH, PIX), BF),
            pltpu.VMEM((REACH, WIDTH, PIX), BF),
            pltpu.VMEM((REACH, WIDTH, PIX), BF),
            pltpu.VMEM((ROWS, WIDTH + 2 * PAD, PIX), BF),
            pltpu.VMEM((ROWS, WIDTH, PIX), F32),
            dma((5,)),
            dma,
            dma((n, 2, 2)),
            dma((n, 2, 2)),
            dma((n, 2)),
            dma((n, 2)),
            dma((n, 2)),
            dma((n, 2)),
            dma((n, 2)),
            dma((n, 2)),
            dma((n,)),
            pltpu.VMEM((REACH, WIDTH, PIX), BF),
            dma((n,)),
            dma((n,)),
        ],
        compiler_params=pltpu.CompilerParams(
            collective_id=0, has_side_effects=True, vmem_limit_bytes=62 * 1024 * 1024
        ),
    )(
        slot_count,
        slot_group[0],
        slot_shift[0],
        density,
        direction,
        inverse_variance,
        pixel_mask,
        block_tiles[0, 0],
    )


def solution(mesh):
    placed = (
        P("tile", None, "los"),
        P("tile", None, "los"),
        P("tile", None, "los"),
        P("tile", None, "los"),
        P("los", "tile"),
        P("los", "tile", None),
        P("los", "tile", None),
        P("los", "tile", None, None, None),
    )
    return jax.shard_map(
        on_device, mesh=mesh, in_specs=placed, out_specs=P("tile", None, "los"), check_vma=False
    )
```

```python
import jax
import jax.numpy as jnp
import numpy as np
from jax import lax
from jax.experimental import pallas as pl
from jax.experimental.pallas import tpu as pltpu
from jax.sharding import PartitionSpec as P

MESH = pl.DeviceIdType.MESH
GROUP = 128
SIGMA = 2
REACH = 6
ROWS = 8
WIDTH = 512
PIX = 128
SLOTS = 128
GROUPS = 32
PAD = 16
CUTS = (0, 128, 256, 384, 512)
SCALE = 2.0**-7
RELAYED = (0,)
TURNED = (2,)
BF = jnp.bfloat16
F32 = jnp.float32


def taps():
    span = np.arange(-REACH, REACH + 1).astype(np.float32)
    values = np.exp(-span * span / np.float32(2.0 * SIGMA * SIGMA)).astype(np.float32)
    held = (values / values.sum(dtype=np.float32)).astype(BF).astype(np.float32)
    return [float(v) for v in held[REACH:]]


def smooth_rows_block(weights, get, put):
    rows = [get(r).astype(F32) for r in range(ROWS + 2 * REACH)]
    for a in range(ROWS):
        mid = a + REACH
        total = weights[0] * rows[mid]
        for k in range(1, REACH + 1):
            total = total + weights[k] * (rows[mid - k] + rows[mid + k])
        put(a, total.astype(BF))


def body(
    cuts,
    cnt_ref,
    grp_ref,
    shf_ref,
    den_ref,
    dir_ref,
    iv_ref,
    msk_ref,
    til_ref,
    out_ref,
    own,
    lo,
    hi,
    rs,
    kc,
    tau,
    mine,
    left,
    right,
    til,
    acc,
    wts,
    tabv,
    tabs,
    iv,
    msk,
    inner,
    send_l,
    send_r,
    got_l,
    got_r,
    pul,
    plo,
    phi,
    br,
    outv,
    load_sem,
    tab_sem,
    p1_send,
    p1_recv,
    p2_send,
    p2_recv,
    p4_send,
    p4_recv,
    p5_send,
    p5_recv,
    out_sem,
    rout,
    hop_send,
    hop_recv,
    side,
    side_send,
    side_recv,
):
    n = len(cuts) - 1
    ycut = [0] + [z + PAD for z in cuts[1:-1]] + [WIDTH]
    vcut = [0] + [z - PAD for z in cuts[1:-1]] + [WIDTH]
    los, tile = lax.axis_index("los"), lax.axis_index("tile")
    n_los, n_tile = lax.axis_size("los"), lax.axis_size("tile")
    nxt = (lax.rem(los + 1, n_los), tile)
    prv = (lax.rem(los + n_los - 1, n_los), tile)
    up = (los, lax.rem(tile + 1, n_tile))
    down = (los, lax.rem(tile + n_tile - 1, n_tile))
    w = taps()
    place, end = lax.rem(tile, n_tile // 2), lax.rem(los, n_los // 2)
    shared = (place < 2) | (place > 5)
    late = (shared & (end == n_los // 2 - 1), shared & (end == 0))
    at_end = (end == n_los // 2 - 1) | (end == 0)
    from_up, from_down = at_end & (place == 7), at_end & (place == 0)
    relay_up, relay_down = at_end & (place == 5), at_end & (place == 2)

    def across(step):
        return (lax.rem(los + n_los // 2, n_los), lax.rem(tile + step, n_tile))

    partners = (
        (from_up, (6, 11)),
        (from_down, (10, 5)),
        (relay_up, (10, 11)),
        (relay_down, (6, 5)),
    )

    middle = jnp.logical_not(shared)
    turn = (middle & (end == n_los // 2 - 1), middle & (end == 0))
    over = jnp.where(end == 0, prv[0], nxt[0])
    beside = lax.rem(tile + jnp.where((place < 2) | (place == 4) | (place == 5), 2, 14), n_tile)

    barrier = pltpu.get_barrier_semaphore()

    @pl.when(at_end)
    def _():
        for other in ((los, beside), (over, beside)):
            pl.semaphore_signal(barrier, inc=1, device_id=other, device_id_type=MESH)

    for other in (nxt, prv, up, down):
        pl.semaphore_signal(barrier, inc=1, device_id=other, device_id_type=MESH)
    for role, steps in partners:

        @pl.when(role)
        def _(steps=steps):
            for step in steps:
                pl.semaphore_signal(barrier, inc=1, device_id=across(step), device_id_type=MESH)

    involved = from_up | from_down | relay_up | relay_down
    pl.semaphore_wait(barrier, jnp.where(involved, 6, 4) + jnp.where(at_end, 2, 0))

    def remote(src, dst, send, recv, device):
        return pltpu.make_async_remote_copy(
            src_ref=src,
            dst_ref=dst,
            send_sem=send,
            recv_sem=recv,
            device_id=device,
            device_id_type=MESH,
        )

    high, low = pl.ds(ROWS - REACH, REACH), pl.ds(0, REACH)

    def launch(role, direct, via):
        if via is None:
            direct.start()
        else:
            pl.when(role)(via.start)
            pl.when(jnp.logical_not(role))(direct.start)

    p1 = []
    for c in range(n):
        ys = pl.ds(ycut[c], ycut[c + 1] - ycut[c])
        copies = []
        for f, src in enumerate((den_ref, dir_ref)):
            for d, (rows, dst, device) in enumerate(((high, lo, up), (low, hi, down))):
                copies.append(
                    remote(
                        src.at[rows, ys],
                        dst.at[f, :, ys],
                        p1_send.at[c, f, d],
                        p1_recv.at[c, f, d],
                        device,
                    )
                )
        for copy in copies:
            copy.start()
        p1.append(copies)

    def pass_on(arrivals, onward):
        for role, copies in zip((relay_up, relay_down), onward):

            @pl.when(role)
            def _(copies=copies):
                for arrival, copy in zip(arrivals, copies):
                    arrival.wait_recv()
                    copy.start()

    def passed(arrivals, onward):
        for role, copies in zip((relay_up, relay_down), onward):

            @pl.when(role)
            def _(copies=copies):
                for copy in copies:
                    copy.wait_send()

    loads = [
        pltpu.make_async_copy(den_ref, own.at[0], load_sem.at[0]),
        pltpu.make_async_copy(dir_ref, own.at[1], load_sem.at[1]),
        pltpu.make_async_copy(til_ref, til, load_sem.at[2]),
        pltpu.make_async_copy(iv_ref, iv, load_sem.at[3]),
        pltpu.make_async_copy(msk_ref, msk, load_sem.at[4]),
    ]
    for load in loads:
        load.start()

    lane = lax.broadcasted_iota(jnp.int32, (SLOTS, SLOTS), 1)
    sub = lax.broadcasted_iota(jnp.int32, (SLOTS, SLOTS), 0)
    count = cnt_ref[0, 0]
    key = (shf_ref[...] + 1) * GROUPS + grp_ref[...]
    key = jnp.where(lax.broadcasted_iota(jnp.int32, (1, SLOTS), 1) < count, key, -1)
    key_row = jnp.broadcast_to(key, (SLOTS, SLOTS))
    key_col = jnp.transpose(key_row)

    def highest(found):
        x = jnp.where(found, sub, -1)
        size = SLOTS
        while size > 8:
            size //= 2
            x = jnp.maximum(x[:size], x[size:])
        for shift in (4, 2, 1):
            x = jnp.maximum(x, pltpu.roll(x, shift, 0))
        return jnp.where(x < 0, SLOTS, x)

    tabv[0] = highest((key_col == key_row) & (sub < lane))
    tabv[1] = highest(key_col == lane)
    to_smem = pltpu.make_async_copy(tabv, tabs, tab_sem)
    to_smem.start()

    rows_i = lax.broadcasted_iota(jnp.int32, kc.shape, 0)
    cols_i = lax.broadcasted_iota(jnp.int32, kc.shape, 1)
    apart = jnp.abs(rows_i + PAD - cols_i)
    band = jnp.zeros(kc.shape, F32)
    for k in range(REACH + 1):
        band = jnp.where(apart == k, w[k], band)
    kc[...] = band.astype(BF)
    for a in range(ROWS):
        for edge in (0, PAD + WIDTH):
            for f in range(2):
                rs[f, a, pl.ds(edge, PAD)] = jnp.zeros((PAD, PIX), BF)
            br[a, pl.ds(edge, PAD)] = jnp.zeros((PAD, PIX), BF)

    loads[0].wait()
    loads[1].wait()

    p2 = []
    for c in range(n):
        for copy in p1[c]:
            copy.wait_recv()
        if c == n - 1:
            for copies in p2:
                for held, copy in zip(late, copies):
                    pl.when(held)(copy.start)

        @pl.loop(0, (ycut[c + 1] - ycut[c]) // 16)
        def _(i, y0=ycut[c]):
            y = pl.multiple_of(y0 + i * 16, 16)
            for f in range(2):

                def get(r):
                    if r < REACH:
                        return lo[f, r, pl.ds(y, 16)]
                    if r < REACH + ROWS:
                        return own[f, r - REACH, pl.ds(y, 16)]
                    return hi[f, r - REACH - ROWS, pl.ds(y, 16)]

                def put(a, value):
                    rs[f, a, pl.ds(y + PAD, 16)] = value

                smooth_rows_block(w, get, put)

        z0, m = cuts[c], cuts[c + 1] - cuts[c]
        zs = pl.ds(z0, m)

        @pl.loop(0, ROWS)
        def _(a, z0=z0, m=m, zs=zs):
            both = jnp.concatenate(
                [rs[0, a, pl.ds(z0, m + 2 * PAD)], rs[1, a, pl.ds(z0, m + 2 * PAD)]], axis=1
            )
            su = jnp.dot(kc[:m, : m + 2 * PAD], both, preferred_element_type=F32)
            t = 0.5 * jnp.exp(1.6 * su[:, :PIX])
            tau[a, zs] = t
            mine[a, 0, zs] = t.astype(BF)
            mine[a, 1, zs] = (1.6 * t * su[:, PIX:]).astype(BF)

        copies = [
            remote(mine.at[:, :, zs], left.at[:, :, zs], p2_send.at[c, 0], p2_recv.at[c, 0], nxt),
            remote(mine.at[:, :, zs], right.at[:, :, zs], p2_send.at[c, 1], p2_recv.at[c, 1], prv),
        ]
        p2.append(copies)
        for d, held in enumerate(late):
            if c < n - 1:
                pl.when(jnp.logical_not(held))(copies[d].start)
            else:
                copies[d].start()

    loads[2].wait()
    to_smem.wait()
    acc[SLOTS] = jnp.zeros((PIX, PIX), F32)

    @pl.loop(0, SLOTS)
    def _(q):
        acc[q] = til[q].astype(F32) * SCALE + acc[tabs[0, 0, q]]

    @pl.loop(0, 3 * GROUPS)
    def _(i):
        wts[i] = acc[tabs[1, 0, i]].astype(BF)

    loads[3].wait()
    loads[4].wait()

    p4, turned = [], []
    per_row = WIDTH // GROUP
    for c in range(n):
        for copy in p2[c]:
            copy.wait_recv()
        z0, m = cuts[c], cuts[c + 1] - cuts[c]
        zs = pl.ds(z0, m)

        @pl.loop(0, ROWS)
        def _(a, zs=zs, m=m, part=z0 // GROUP):
            g = a * per_row + part
            total = None
            for o, ref in enumerate((left, mine, right)):
                block = jnp.concatenate([ref[a, 0, zs], ref[a, 1, zs]], axis=0)
                term = jnp.dot(block, wts[o * GROUPS + g], preferred_element_type=F32)
                total = term if total is None else total + term
            total = total * (1.0 / SCALE)
            flux = jnp.exp(-total[:m])
            weight = msk[a, zs].astype(F32) * iv[a, zs].astype(F32)
            adjoint = (weight * flux * flux * total[m:]).astype(BF)
            back = [
                lax.dot_general(
                    adjoint,
                    wts[o * GROUPS + g],
                    (((1,), (1,)), ((), ())),
                    preferred_element_type=F32,
                )
                * (1.0 / SCALE)
                for o in range(3)
            ]
            send_l[a, zs] = back[0].astype(BF)
            inner[a, zs] = back[1]
            send_r[a, zs] = back[2].astype(BF)

        copies = []
        for d, (src, dst, device) in enumerate(((send_r, got_l, nxt), (send_l, got_r, prv))):
            sems = (p4_send.at[c, d], p4_recv.at[c, d])
            direct = remote(src.at[:, zs], dst.at[:, zs], *sems, device)
            via = None
            if c in TURNED:
                kept = side.at[:, zs]
                via = remote(src.at[:, zs], kept, sems[0], side_recv.at[c], (los, beside))
                on = remote(kept, dst.at[:, zs], side_send.at[c], sems[1], (over, beside))
                turned.append((turn[d], via, on))
            launch(late[d], direct, via)
            copies.append(direct)
        p4.append(copies)

    for role, via, on in turned:

        @pl.when(role)
        def _(via=via, on=on):
            via.wait_recv()
            on.start()

    p5 = []
    outs = []
    back = []

    def finish(c):
        for copy in p5[c]:
            copy.wait_recv()

        @pl.loop(0, (cuts[c + 1] - cuts[c]) // 16)
        def _(i):
            y = pl.multiple_of(cuts[c] + i * 16, 16)

            def get(r):
                if r < REACH:
                    return plo[r, pl.ds(y, 16)]
                if r < REACH + ROWS:
                    return pul[r - REACH, pl.ds(y, 16)]
                return phi[r - REACH - ROWS, pl.ds(y, 16)]

            def put(a, value):
                br[a, pl.ds(y + PAD, 16)] = value

            smooth_rows_block(w, get, put)

        v0, m = vcut[c], vcut[c + 1] - vcut[c]

        @pl.loop(0, ROWS)
        def _(a):
            outv[a, pl.ds(v0, m)] = jnp.dot(
                kc[:m, : m + 2 * PAD], br[a, pl.ds(v0, m + 2 * PAD)], preferred_element_type=F32
            )

        copy = pltpu.make_async_copy(
            outv.at[:, pl.ds(v0, m)], out_ref.at[:, pl.ds(v0, m)], out_sem.at[c]
        )
        copy.start()
        outs.append(copy)

    for c in range(n):
        for copy in p4[c]:
            copy.wait_recv()
        zs = pl.ds(cuts[c], cuts[c + 1] - cuts[c])

        @pl.loop(0, ROWS)
        def _(a, zs=zs):
            real = inner[a, zs] + got_l[a, zs].astype(F32) + got_r[a, zs].astype(F32)
            pul[a, zs] = (1.6 * tau[a, zs] * real).astype(BF)

        copies, arrivals, onward = [], [], ([], [])
        for d, (rows, dst, device, role, step) in enumerate(
            ((high, plo, up, from_up, 6), (low, phi, down, from_down, 10))
        ):
            sems = (p5_send.at[c, d], p5_recv.at[c, d])
            direct = remote(pul.at[rows, zs], dst.at[:, zs], *sems, device)
            via = None
            if c in RELAYED:
                kept = rout.at[:, zs]
                via = remote(pul.at[rows, zs], kept, sems[0], hop_recv.at[c], across(step))
                goal = across((11, 5)[d])
                onward[d].append(remote(kept, dst.at[:, zs], hop_send.at[c], sems[1], goal))
                if d == 0:
                    arrivals.append(via)
            launch(role, direct, via)
            copies.append(direct)
        p5.append(copies)
        if arrivals:
            back.append((arrivals, onward))
    for relayed in back:
        pass_on(*relayed)
    for c in range(n):
        finish(c)
    for group in (p1, p2, p4, p5):
        for copies in group:
            for copy in copies:
                copy.wait_send()
    for relayed in back:
        passed(*relayed)
    for role, _, on in turned:
        pl.when(role)(on.wait_send)
    for copy in outs:
        copy.wait()


def on_device(
    density,
    direction,
    inverse_variance,
    pixel_mask,
    slot_count,
    slot_group,
    slot_shift,
    block_tiles,
):
    cuts = CUTS
    n = len(cuts) - 1
    tallest = max([b - a for a, b in zip(cuts, cuts[1:])] + [WIDTH - cuts[-2] + PAD])
    any_spec = pl.BlockSpec(memory_space=pl.ANY)
    vmem = pl.BlockSpec(memory_space=pltpu.VMEM)
    dma = pltpu.SemaphoreType.DMA

    def kernel(*refs):
        body(cuts, *refs)

    return pl.pallas_call(
        kernel,
        name="hessian_product",
        out_shape=jax.ShapeDtypeStruct((ROWS, WIDTH, PIX), F32),
        in_specs=[
            pl.BlockSpec(memory_space=pltpu.SMEM),
            vmem,
            vmem,
            any_spec,
            any_spec,
            any_spec,
            any_spec,
            any_spec,
        ],
        out_specs=any_spec,
        scratch_shapes=[
            pltpu.VMEM((2, ROWS, WIDTH, PIX), BF),
            pltpu.VMEM((2, REACH, WIDTH, PIX), BF),
            pltpu.VMEM((2, REACH, WIDTH, PIX), BF),
            pltpu.VMEM((2, ROWS, WIDTH + 2 * PAD, PIX), BF),
            pltpu.VMEM((tallest, 256), BF),
            pltpu.VMEM((ROWS, WIDTH, PIX), F32),
            pltpu.VMEM((ROWS, 2, WIDTH, PIX), BF),
            pltpu.VMEM((ROWS, 2, WIDTH, PIX), BF),
            pltpu.VMEM((ROWS, 2, WIDTH, PIX), BF),
            pltpu.VMEM((SLOTS, PIX, PIX), BF),
            pltpu.VMEM((SLOTS + 1, PIX, PIX), F32),
            pltpu.VMEM((3 * GROUPS, PIX, PIX), BF),
            pltpu.VMEM((2, 8, SLOTS), jnp.int32),
            pltpu.SMEM((2, 8, SLOTS), jnp.int32),
            pltpu.VMEM((ROWS, WIDTH, PIX), BF),
            pltpu.VMEM((ROWS, WIDTH, PIX), jnp.int32),
            pltpu.VMEM((ROWS, WIDTH, PIX), F32),
            pltpu.VMEM((ROWS, WIDTH, PIX), BF),
            pltpu.VMEM((ROWS, WIDTH, PIX), BF),
            pltpu.VMEM((ROWS, WIDTH, PIX), BF),
            pltpu.VMEM((ROWS, WIDTH, PIX), BF),
            pltpu.VMEM((ROWS, WIDTH, PIX), BF),
            pltpu.VMEM((REACH, WIDTH, PIX), BF),
            pltpu.VMEM((REACH, WIDTH, PIX), BF),
            pltpu.VMEM((ROWS, WIDTH + 2 * PAD, PIX), BF),
            pltpu.VMEM((ROWS, WIDTH, PIX), F32),
            dma((5,)),
            dma,
            dma((n, 2, 2)),
            dma((n, 2, 2)),
            dma((n, 2)),
            dma((n, 2)),
            dma((n, 2)),
            dma((n, 2)),
            dma((n, 2)),
            dma((n, 2)),
            dma((n,)),
            pltpu.VMEM((REACH, WIDTH, PIX), BF),
            dma((n,)),
            dma((n,)),
            pltpu.VMEM((ROWS, WIDTH, PIX), BF),
            dma((n,)),
            dma((n,)),
        ],
        compiler_params=pltpu.CompilerParams(
            collective_id=0, has_side_effects=True, vmem_limit_bytes=62 * 1024 * 1024
        ),
    )(
        slot_count,
        slot_group[0],
        slot_shift[0],
        density,
        direction,
        inverse_variance,
        pixel_mask,
        block_tiles[0, 0],
    )


def solution(mesh):
    placed = (
        P("tile", None, "los"),
        P("tile", None, "los"),
        P("tile", None, "los"),
        P("tile", None, "los"),
        P("los", "tile"),
        P("los", "tile", None),
        P("los", "tile", None),
        P("los", "tile", None, None, None),
    )
    return jax.shard_map(
        on_device, mesh=mesh, in_specs=placed, out_specs=P("tile", None, "los"), check_vma=False
    )
```
